256 devices in a mesh: dp: 8 (over z_lo, core), vocab: 32 (over y, x, z_hi).
Axes of the slice: x: 4, y: 4, z: 8 (z_hi: 2, z_lo: 4; z = z_hi * 4 + z_lo), core: 2. Of those that a mesh axis runs over, the one named last changes fastest.
Arguments:
- table: bfloat16 [32768, 4096], P('vocab'), may hold values from -0.75 to 0.75
- hidden: bfloat16 [2048, 4096], P(('dp', 'vocab')), may hold values from -9 to 9
- cotangent: bfloat16 [2048, 4096], P(('dp', 'vocab')), may hold values from -0.75 to 0.75
- input_ids: int32 [2048], P('dp'), may hold values from 0 to 32767, as said below
- target_ids: int32 [2048], P('dp'), may hold values from 0 to 32767
Outputs:
- table_grad: float32 [32768, 4096], P(('vocab', 'dp'))
- hidden_grad: bfloat16 [2048, 4096], P(('dp', 'vocab'))
- token_loss: float32 [2048], P('dp')
The draws below stay inside these ranges and needn't reach their ends.
Inputs may be any that keep to these rules, and one draw needn't show every extreme that they name: `input_ids`: the ids of one replica group may all lie in the 1024 rows of one index of vocab; in every draw some group's ids do.
All inputs are finite; a program needn't handle non-finite values.
Results may differ from the reference program's by a relative error of at most 0.0034.
Values may be sent and summed in bfloat16 or wider, within the bound.
No kernel may reach another device: no remote copies, remote signals or barrier semaphores. Data moves between devices by JAX's collectives and lax.ppermute only.
A program may use at most 128 MiB of HBM per device.

```python
import jax
import jax.numpy as jnp
from jax import lax

D = 4096
V_DEV = 1024
MICRO = 8
MB_ROWS = 32
GROUP = 256
V = 32768
TOKENS = 2048
N_DP = 8


def table_values(key):
    base = jax.random.normal(jax.random.fold_in(key, 11), (V, D), jnp.float32) * 0.125
    return jnp.clip(base, -0.75, 0.75)


def draw_table(key, part):
    return table_values(key).astype(jnp.bfloat16)


def draw_hidden(key, part):
    scales = jnp.exp(jax.random.uniform(jax.random.fold_in(key, 13), (TOKENS, 1), jnp.float32, jnp.log(0.12), jnp.log(0.5)))
    base = jax.random.normal(jax.random.fold_in(key, 12), (TOKENS, D), jnp.float32)
    return jnp.clip(base * scales, -8.0, 8.0).astype(jnp.bfloat16)


def draw_input_ids(key, part):
    groups = TOKENS // GROUP
    shards = V // V_DEV
    hot_group = jax.random.randint(jax.random.fold_in(key, 21), (), 0, groups)
    hot_shard = jax.random.randint(jax.random.fold_in(key, 22), (groups, 1), 0, shards)
    levels = jax.random.randint(jax.random.fold_in(key, 23), (groups, 1), 0, 5)
    group_index = jnp.arange(groups, dtype=jnp.int32)[:, None]
    levels = jnp.where(group_index == hot_group, 4, levels)
    pickers = jax.random.randint(jax.random.fold_in(key, 24), (groups, GROUP), 0, 4)
    concentrated = pickers < levels
    in_shard = hot_shard * V_DEV + jax.random.randint(jax.random.fold_in(key, 25), (groups, GROUP), 0, V_DEV)
    anywhere = jax.random.randint(jax.random.fold_in(key, 26), (groups, GROUP), 0, V)
    values = jnp.where(concentrated, in_shard, anywhere)
    return values.reshape(TOKENS).astype(jnp.int32)


def plant(values, stream_key, smallest, largest):
    shape = values.shape
    index_at = [jax.random.randint(jax.random.fold_in(stream_key, axis), (), 0, shape[axis]) for axis in range(len(shape))]
    values = values.at[tuple(index_at)].set(smallest)
    longest = shape.index(max(shape))
    index_at[longest] = (index_at[longest] + 1) % shape[longest]
    return values.at[tuple(index_at)].set(largest)


def shard_levels(own_key, dims, split, smallest, largest):
    def one(axis_at, parts):
        heights = jax.random.uniform(jax.random.fold_in(jax.random.fold_in(own_key, 6), axis_at), (parts,), jnp.float32, smallest / len(split), largest / len(split))
        return jnp.repeat(jnp.exp(heights), dims[axis_at] // parts).reshape((-1,) + (1,) * (len(dims) - axis_at - 1))

    loudness = one(*split[0])
    for cut in split[1:]:
        loudness = loudness * one(*cut)
    return loudness


def centred(stream_key, extent, deviation, reach, cuts=(), kind=jnp.bfloat16):
    values = jax.random.normal(stream_key, extent, jnp.float32) * deviation
    if len(cuts) > 0:
        values = shard_levels(stream_key, extent, cuts, -0.22, 0.18) * values
    return jnp.clip(values, min=-reach, max=reach).astype(kind)


def setup_inputs(seed: int = 0) -> dict:
    keys = jax.random.split(jax.random.key(seed), 6)
    return {
        "table": draw_table(jax.random.fold_in(keys[5], 71), 0),
        "hidden": draw_hidden(jax.random.fold_in(keys[5], 71), 0),
        "cotangent": centred(keys[2], (TOKENS, D), 0.05, 0.75, ((0, 256),)),
        "input_ids": draw_input_ids(jax.random.fold_in(keys[5], 71), 0),
        "target_ids": plant(jax.random.randint(keys[4], (TOKENS,), 0, V), jax.random.fold_in(keys[4], 1), 0, V - 1).astype(jnp.int32),
    }


def reference(table, hidden, cotangent, input_ids, target_ids):
    group = MICRO * MB_ROWS
    vocab_rows = table.shape[0]
    width = table.shape[1]
    columns = jnp.arange(vocab_rows, dtype=jnp.int32)

    def one_group(total, index):
        begin = (index * group).astype(jnp.int32)
        rows = lax.dynamic_slice_in_dim(hidden, begin, group, 0)
        incoming = lax.dynamic_slice_in_dim(cotangent, begin, group, 0)
        inputs = lax.dynamic_slice_in_dim(input_ids, begin, group, 0)
        targets = lax.dynamic_slice_in_dim(target_ids, begin, group, 0)
        logits = lax.dot_general(rows, table, (((1,), (1,)), ((), ())), preferred_element_type=jnp.float32)
        top = jnp.max(logits, axis=1)
        lse = top + jnp.log(jnp.sum(jnp.exp(logits - top[:, None]), axis=1))
        hit = targets[:, None] == columns[None, :]
        picked = jnp.sum(jnp.where(hit, logits, jnp.float32(0.0)), axis=1)
        loss = lse - picked
        probs = jnp.exp(logits - lse[:, None])
        dlogits = (probs - hit.astype(jnp.float32)).astype(jnp.bfloat16)
        row_grad = jnp.dot(dlogits, table, preferred_element_type=jnp.float32).astype(jnp.bfloat16)
        grad = lax.dot_general(dlogits, rows, (((0,), (0,)), ((), ())), preferred_element_type=jnp.float32)
        grad = grad.at[inputs].add(incoming.astype(jnp.float32))
        return total + grad, (row_grad, loss)

    start = jnp.zeros((vocab_rows, width), jnp.float32)
    total, (row_grads, losses) = lax.scan(one_group, start, jnp.arange(N_DP, dtype=jnp.int32))
    return total, row_grads.reshape(-1, width), losses.reshape(-1)
```

```python
import jax
import jax.numpy as jnp
from jax import lax
from jax.sharding import Mesh
from jax.sharding import PartitionSpec as P

VOCAB = ("y", "x", "h")
DP = ("za", "zb", "c")
F32 = jnp.float32
BF16 = jnp.bfloat16
EXACT = lax.Precision.HIGHEST


def shift(array, axis, by):
    n = lax.axis_size(axis)
    return lax.ppermute(array, axis, [(i, (i + by) % n) for i in range(n)])


def swap(array, axis):
    n = lax.axis_size(axis)
    return lax.ppermute(array, axis, [(i, n - 1 - i) for i in range(n)])


def joined(pieces, parts):
    size = pieces[0].shape[0] // parts
    return jnp.concatenate(
        [piece[t * size : (t + 1) * size] for t in range(parts) for piece in pieces]
    )


def around(array, axis):
    return [array] + [shift(array, axis, k) for k in range(1, lax.axis_size(axis))]


def plane_gather(first, second, parts):
    along_x = joined(around(first, "x"), parts)
    along_y = joined(around(second, "y"), parts)
    return around(along_x, "y"), around(along_y, "x")


def sum_back(blocks, axis, dtype):
    total = blocks[0]
    for k in range(1, len(blocks)):
        total = total + shift(blocks[k].astype(dtype), axis, -k).astype(F32)
    return total


def cut(array, count):
    size = array.shape[0] // count
    return [array[k * size : (k + 1) * size] for k in range(count)]


def shards(table, hidden, cotangent, input_ids, target_ids):
    shard_rows, width = table.shape
    block = hidden.shape[0]
    group = input_ids.shape[0]
    half_rows = shard_rows // 2
    y, x, h = (lax.axis_index(name) for name in VOCAB)
    za, zb, c = (lax.axis_index(name) for name in DP)
    ny, nx = lax.axis_size("y"), lax.axis_size("x")
    offset = lax.axis_index(VOCAB) * shard_rows
    half = za * half_rows

    at = jnp.arange(group, dtype=jnp.int32)
    path = at // (group // 2)
    outer = at // (group // 2 // ny) % ny
    inner = at // block % nx
    behind_y = jnp.where(path == 0, outer, inner)
    behind_x = jnp.where(path == 0, inner, outer)
    owner = ((y - behind_y) % ny * nx + (x - behind_x) % nx) * 2 + (h + path) % 2
    token = owner * block + at % block
    order = (token[:, None] == jnp.arange(group, dtype=jnp.int32)[None, :]).astype(F32)

    ids = jnp.stack([input_ids, target_ids])
    ids_both = jnp.concatenate([ids, swap(ids, "za")])
    ids_local = jnp.dot(ids_both.astype(F32), order.T, precision=EXACT).astype(jnp.int32)
    own_in, own_target, other_in, other_target = ids_local

    rows0, rows1 = plane_gather(hidden, swap(hidden, "h"), 1)
    rows = jnp.concatenate(rows0 + rows1)

    both = jnp.concatenate([hidden, cotangent])
    far0, far1 = swap(both, "za"), lax.ppermute(both, ("za", "h"), [(0, 3), (3, 0), (1, 2), (2, 1)])
    near1 = swap(cotangent, "h")
    first = jnp.concatenate([far0[:block], cotangent, far0[block:]])
    second = jnp.concatenate([far1[:block], near1, far1[block:]])
    more0, more1 = plane_gather(first, second, 3)
    third = more0[0].shape[0] // 3
    more = jnp.concatenate(
        [piece[t * third : (t + 1) * third] for t in range(3) for side in (more0, more1) for piece in side]
    )
    other_rows = more[:group]

    logits = lax.dot_general(rows, table, (((1,), (1,)), ((), ())), preferred_element_type=F32)
    columns = offset + jnp.arange(shard_rows, dtype=jnp.int32)
    hit = own_target[:, None] == columns[None, :]
    local_pick = jnp.sum(jnp.where(hit, logits, F32(0.0)), axis=1)
    local_max = jnp.max(logits, axis=1)
    local_total = jnp.sum(jnp.exp(logits - local_max[:, None]), axis=1)
    mine = jnp.dot(jnp.stack([local_max, local_total, local_pick]), order, precision=EXACT)
    everyone = lax.all_to_all(
        jnp.broadcast_to(mine, (lax.axis_size(VOCAB), *mine.shape)), VOCAB, 0, 0, tiled=True
    )
    top = jnp.max(everyone[:, 0], axis=0)
    total = jnp.sum(everyone[:, 1] * jnp.exp(everyone[:, 0] - top), axis=0)
    lse = top + jnp.log(total)
    token_loss = lse - jnp.sum(everyone[:, 2], axis=0)

    lse_both = jnp.dot(jnp.stack([lse, swap(lse, "za")]), order.T, precision=EXACT)
    dlogits = (jnp.exp(logits - lse_both[0][:, None]) - hit.astype(F32)).astype(BF16)

    partial = jnp.dot(dlogits, table, preferred_element_type=F32)
    part0, part1 = cut(partial, 2)
    part0 = sum_back(cut(sum_back(cut(part0, ny), "y", BF16), nx), "x", F32)
    part1 = sum_back(cut(sum_back(cut(part1, nx), "x", BF16), ny), "y", F32)
    hidden_grad = (part0 + swap(part1, "h")).astype(BF16)

    half_table = lax.dynamic_slice_in_dim(table, half, half_rows, 0)
    half_columns = offset + half + jnp.arange(half_rows, dtype=jnp.int32)
    other_logits = lax.dot_general(
        other_rows, half_table, (((1,), (1,)), ((), ())), preferred_element_type=F32
    )
    other_hit = other_target[:, None] == half_columns[None, :]
    other_dlogits = (jnp.exp(other_logits - lse_both[1][:, None]) - other_hit.astype(F32)).astype(BF16)
    inputs = jnp.concatenate([own_in, other_in])
    picks = (inputs[:, None] == half_columns[None, :]).astype(BF16)
    left = jnp.concatenate([other_dlogits, picks])
    own_dlogits = lax.dynamic_slice_in_dim(dlogits, half, half_rows, 1)
    contract = (((0,), (0,)), ((), ()))
    grad = lax.dot_general(left, more, contract, preferred_element_type=F32) + lax.dot_general(
        own_dlogits, rows, contract, preferred_element_type=F32
    )
    grad = grad.reshape(2, 2, half_rows // 4, width)
    take = lambda array, at, dim: lax.dynamic_index_in_dim(array, at, dim, keepdims=False)
    grad = take(grad, c, 1) + swap(take(grad, 1 - c, 1).astype(BF16), "c").astype(F32)
    table_grad = take(grad, zb, 0) + swap(take(grad, 1 - zb, 0).astype(BF16), "zb").astype(F32)
    return (table_grad, hidden_grad, token_loss)


def solution(mesh):
    finer = Mesh(mesh.devices.reshape(2, 2, 2, 4, 4, 2), DP + VOCAB)
    in_specs = (P(VOCAB, None), P(DP + VOCAB, None), P(DP + VOCAB, None), P(DP), P(DP))
    out_specs = (P(VOCAB + DP, None), P(DP + VOCAB, None), P(DP))
    return jax.shard_map(
        shards, mesh=finer, in_specs=in_specs, out_specs=out_specs, check_vma=False
    )
```

```python
import jax
import jax.numpy as jnp
from jax import lax
from jax.experimental import pallas as pl
from jax.experimental.pallas import tpu as pltpu
from jax.sharding import Mesh
from jax.sharding import PartitionSpec as P

VOCAB = ("y", "x", "h")
DP = ("za", "zb", "c")
F32 = jnp.float32
BF16 = jnp.bfloat16
CHUNKS = 2
EXACT = lax.Precision.HIGHEST


def after(value, *others):
    return lax.optimization_barrier((value, *others))[0]


def shift(array, axis, by):
    n = lax.axis_size(axis)
    return lax.ppermute(array, axis, [(i, (i + by) % n) for i in range(n)])


def swap(array, axis):
    n = lax.axis_size(axis)
    return lax.ppermute(array, axis, [(i, n - 1 - i) for i in range(n)])


def take(array, at, dim):
    return lax.dynamic_index_in_dim(array, at, dim, keepdims=False)


def ordered(array, zb, c, dim):
    by_core = [take(array, core, dim + 1) for core in (c, 1 - c)]
    return jnp.stack([jnp.stack([take(a, z, dim) for z in (zb, 1 - zb)], dim) for a in by_core], dim)


def table_product_kernel(own_ref, left_ref, rows_ref, more_ref, keep_ref, send_ref):
    contract = (((0,), (0,)), ((), ()))
    total = lax.dot_general(left_ref[...], more_ref[...], contract, preferred_element_type=F32)
    total += lax.dot_general(own_ref[...], rows_ref[...], contract, preferred_element_type=F32)
    half = total.shape[0] // 2
    keep_ref[...] = total[:half]
    send_ref[...] = total[half:].astype(BF16)


def table_product(own, left, rows, more, at_column, columns):
    tokens, out_rows = own.shape
    depth = more.shape[0]
    tile = min(512, columns)
    begin = at_column // tile
    still = lambda i: (0, 0)
    moving = lambda i: (0, begin + i)
    return pl.pallas_call(
        table_product_kernel,
        grid=(columns // tile,),
        in_specs=[
            pl.BlockSpec((tokens, out_rows), still),
            pl.BlockSpec((depth, out_rows), still),
            pl.BlockSpec((tokens, tile), moving),
            pl.BlockSpec((depth, tile), moving),
        ],
        out_specs=[pl.BlockSpec((out_rows // 2, tile), lambda i: (0, i))] * 2,
        out_shape=[
            jax.ShapeDtypeStruct((out_rows // 2, columns), F32),
            jax.ShapeDtypeStruct((out_rows // 2, columns), BF16),
        ],
        compiler_params=pltpu.CompilerParams(vmem_limit_bytes=32 << 20),
        cost_estimate=pl.CostEstimate(
            flops=2 * (tokens + depth) * out_rows * columns,
            bytes_accessed=2 * (tokens + depth) * (out_rows + columns) + 3 * out_rows * columns,
            transcendentals=0,
        ),
    )(own, left, rows, more)


def around(array, axis):
    return [array] + [shift(array, axis, k) for k in range(1, lax.axis_size(axis))]


def sum_back(blocks, axis, dtype):
    total = blocks[0]
    for k in range(1, len(blocks)):
        total = total + shift(blocks[k].astype(dtype), axis, -k).astype(F32)
    return total


def cut(array, count):
    size = array.shape[0] // count
    return [array[k * size : (k + 1) * size] for k in range(count)]


def shards(table, hidden, cotangent, input_ids, target_ids):
    shard_rows, width = table.shape
    block = hidden.shape[0]
    group = input_ids.shape[0]
    half_rows = shard_rows // 2
    y, x, h = (lax.axis_index(name) for name in VOCAB)
    za, zb, c = (lax.axis_index(name) for name in DP)
    ny, nx = lax.axis_size("y"), lax.axis_size("x")
    offset = lax.axis_index(VOCAB) * shard_rows
    half = za * half_rows

    at = jnp.arange(group, dtype=jnp.int32)
    path = at // (group // 2)
    outer = at // (group // 2 // ny) % ny
    inner = at // block % nx
    behind_y = jnp.where(path == 0, outer, inner)
    behind_x = jnp.where(path == 0, inner, outer)
    owner = ((y - behind_y) % ny * nx + (x - behind_x) % nx) * 2 + (h + path) % 2
    token = owner * block + at % block
    order = (token[:, None] == jnp.arange(group, dtype=jnp.int32)[None, :]).astype(F32)

    own_target = jnp.dot(order, target_ids.astype(F32), precision=EXACT).astype(jnp.int32)

    both = jnp.concatenate([hidden, cotangent])
    near = swap(both, "h")
    far = [swap(both, "za"), lax.ppermute(both, ("za", "h"), [(0, 3), (3, 0), (1, 2), (2, 1)])]
    along_x = around(hidden, "x")
    near, *far = lax.optimization_barrier((near, *far, *along_x[1:]))[:3]
    sends = jnp.concatenate([*far, near[block:], cotangent])
    more = lax.all_gather(sends, ("y", "x"), axis=0, tiled=True)

    along_x = after(jnp.concatenate(along_x), sends)
    rows0 = around(along_x, "y")
    along_y = jnp.concatenate(around(near[:block], "y"))
    rows1 = around(along_y, "x")
    rows = jnp.concatenate(rows0 + rows1)
    other_ids = swap(input_ids, "za")

    logits = lax.dot_general(rows, table, (((1,), (1,)), ((), ())), preferred_element_type=F32)
    columns = offset + jnp.arange(shard_rows, dtype=jnp.int32)
    hit = own_target[:, None] == columns[None, :]
    local_pick = jnp.sum(jnp.where(hit, logits, F32(0.0)), axis=1)
    local_max = jnp.max(logits, axis=1)
    local_total = jnp.sum(jnp.exp(logits - local_max[:, None]), axis=1)
    mine = jnp.dot(jnp.stack([local_max, local_total, local_pick]), order, precision=EXACT)
    everyone = lax.all_to_all(
        jnp.broadcast_to(mine, (lax.axis_size(VOCAB), *mine.shape)), VOCAB, 0, 0, tiled=True
    )
    top = jnp.max(everyone[:, 0], axis=0)
    total = jnp.sum(everyone[:, 1] * jnp.exp(everyone[:, 0] - top), axis=0)
    lse = top + jnp.log(total)
    token_loss = lse - jnp.sum(everyone[:, 2], axis=0)

    lse_local = jnp.dot(order, lse, precision=EXACT)
    dlogits = (jnp.exp(logits - lse_local[:, None]) - hit.astype(F32)).astype(BF16)
    chips, quarter = ny * nx, half_rows // 4
    by_place = dlogits.reshape(group, 2, 2, 2, quarter)
    own_dlogits, for_other = (
        ordered(take(by_place, side, 1), zb, c, 1).reshape(group, half_rows) for side in (za, 1 - za)
    )
    for_other = jnp.dot(order.T.astype(BF16), for_other, preferred_element_type=F32)
    for_other = for_other.astype(BF16)
    other_dlogits = swap(for_other, "za")

    partial = jnp.dot(after(dlogits, for_other), table, preferred_element_type=F32)
    part0, part1 = cut(partial, 2)
    part0 = sum_back(cut(part0, ny), "y", BF16)
    part1 = sum_back(cut(part1, nx), "x", BF16)

    half_columns = ordered(
        (offset + half + jnp.arange(half_rows, dtype=jnp.int32)).reshape(2, 2, quarter), zb, c, 0
    ).reshape(half_rows)
    picks = [(ids[:, None] == half_columns[None, :]).astype(BF16) for ids in (input_ids, other_ids)]
    sides = []
    for part in (other_dlogits, picks[1], picks[0]):
        part = part.reshape(chips, 2, block, half_rows)
        sides.append([jnp.where(h == side, part[:, 0], part[:, 1]) for side in (0, 1)])
    left = [sides[0][0], sides[1][0], sides[0][1], sides[1][1], sides[2][1], sides[2][0]]
    left = jnp.concatenate(left, axis=1).reshape(-1, half_rows)
    pieces = []
    for at_column in range(0, width, width // CHUNKS):
        keep, send = table_product(own_dlogits, left, rows, more, at_column, width // CHUNKS)
        got = swap(send, "c")
        mine, theirs = (k + g.astype(F32) for k, g in zip(cut(keep, 2), cut(got, 2)))
        theirs = theirs.astype(BF16)
        pieces.append((mine, swap(theirs, "zb")))
    table_grad = jnp.concatenate([mine + got.astype(F32) for mine, got in pieces], axis=1)

    part0, part1 = (after(part, theirs) for part in (part0, part1))
    part0 = sum_back(cut(part0, nx), "x", F32)
    part1 = sum_back(cut(part1, ny), "y", F32)
    hidden_grad = (part0 + swap(part1, "h")).astype(BF16)
    return (table_grad, hidden_grad, token_loss)


def solution(mesh):
    finer = Mesh(mesh.devices.reshape(2, 2, 2, 4, 4, 2), DP + VOCAB)
    in_specs = (P(VOCAB, None), P(DP + VOCAB, None), P(DP + VOCAB, None), P(DP), P(DP))
    out_specs = (P(VOCAB + DP, None), P(DP + VOCAB, None), P(DP))
    return jax.shard_map(
        shards, mesh=finer, in_specs=in_specs, out_specs=out_specs, check_vma=False
    )
```

```python
import functools

import jax
import jax.numpy as jnp
from jax import lax
from jax.experimental import pallas as pl
from jax.experimental.pallas import tpu as pltpu
from jax.sharding import Mesh
from jax.sharding import PartitionSpec as P

VOCAB = ("y", "x", "h")
DP = ("za", "zb", "c")
F32 = jnp.float32
BF16 = jnp.bfloat16
CHUNKS = 2
EXACT = lax.Precision.HIGHEST


def after(value, *others):
    return lax.optimization_barrier((value, *others))[0]


def shift(array, axis, by):
    n = lax.axis_size(axis)
    return lax.ppermute(array, axis, [(i, (i + by) % n) for i in range(n)])


def swap(array, axis):
    n = lax.axis_size(axis)
    return lax.ppermute(array, axis, [(i, n - 1 - i) for i in range(n)])


def hidden_product_kernel(weights_ref, hit_ref, table_ref, sum_ref, target_ref):
    left = jnp.concatenate([weights_ref[...], hit_ref[...]])
    both = jnp.dot(left, table_ref[...], preferred_element_type=F32)
    tokens = sum_ref.shape[0]
    sum_ref[...] = both[:tokens]
    target_ref[...] = both[tokens:].astype(BF16)


def hidden_product(weights, hit, table):
    tokens, depth = weights.shape
    columns = table.shape[1]
    tile = min(512, columns)
    still = pl.BlockSpec((tokens, depth), lambda i: (0, 0))
    out = pl.BlockSpec((tokens, tile), lambda i: (0, i))
    return pl.pallas_call(
        hidden_product_kernel,
        grid=(columns // tile,),
        in_specs=[still, still, pl.BlockSpec((depth, tile), lambda i: (0, i))],
        out_specs=[out, out],
        out_shape=[jax.ShapeDtypeStruct((tokens, columns), kind) for kind in (F32, BF16)],
        compiler_params=pltpu.CompilerParams(vmem_limit_bytes=56 << 20),
        cost_estimate=pl.CostEstimate(
            flops=4 * tokens * depth * columns,
            bytes_accessed=2 * depth * (2 * tokens + columns) + 6 * tokens * columns,
            transcendentals=0,
        ),
    )(weights, hit, table)


def table_product_kernel(chips, own_ref, other_ref, picks_ref, rows_ref, more_ref, keep_ref, send_ref):
    contract = (((0,), (0,)), ((), ()))
    tile = more_ref.shape[1]
    more = more_ref[...].reshape(chips, -1, tile)
    split = other_ref.shape[0] // chips
    total = lax.dot_general(own_ref[...], rows_ref[...], contract, preferred_element_type=F32)
    for left, right in ((other_ref, more[:, :split]), (picks_ref, more[:, split:])):
        right = right.reshape(-1, tile)
        total += lax.dot_general(left[...], right, contract, preferred_element_type=F32)
    half = total.shape[0] // 2
    keep_ref[...] = total[:half]
    send_ref[...] = total[half:].astype(BF16)


def table_product(own, other, picks, rows, more, at_column, columns):
    tokens, out_rows = own.shape
    depth = more.shape[0]
    chips = lax.axis_size(("y", "x"))
    tile = min(512, columns)
    begin = at_column // tile
    still = lambda i: (0, 0)
    moving = lambda i: (0, begin + i)
    return pl.pallas_call(
        functools.partial(table_product_kernel, chips),
        grid=(columns // tile,),
        in_specs=[
            pl.BlockSpec((tokens, out_rows), still),
            pl.BlockSpec((tokens, out_rows), still),
            pl.BlockSpec((depth - tokens, out_rows), still),
            pl.BlockSpec((tokens, tile), moving),
            pl.BlockSpec((depth, tile), moving),
        ],
        out_specs=[pl.BlockSpec((out_rows // 2, tile), lambda i: (0, i))] * 2,
        out_shape=[
            jax.ShapeDtypeStruct((out_rows // 2, columns), F32),
            jax.ShapeDtypeStruct((out_rows // 2, columns), BF16),
        ],
        compiler_params=pltpu.CompilerParams(vmem_limit_bytes=56 << 20),
        cost_estimate=pl.CostEstimate(
            flops=2 * (tokens + depth) * out_rows * columns,
            bytes_accessed=2 * (tokens + depth) * (out_rows + columns) + 3 * out_rows * columns,
            transcendentals=0,
        ),
    )(own, other, picks, rows, more)


def around(array, axis):
    return [array] + [shift(array, axis, k) for k in range(1, lax.axis_size(axis))]


def cut(array, count):
    size = array.shape[0] // count
    return [array[k * size : (k + 1) * size] for k in range(count)]


def shards(table, hidden, cotangent, input_ids, target_ids):
    shard_rows, width = table.shape
    block = hidden.shape[0]
    group = input_ids.shape[0]
    half_rows = shard_rows // 2
    y, x, h = (lax.axis_index(name) for name in VOCAB)
    za, zb, c = (lax.axis_index(name) for name in DP)
    ny, nx = lax.axis_size("y"), lax.axis_size("x")
    offset = lax.axis_index(VOCAB) * shard_rows
    half = za * half_rows

    at = jnp.arange(group, dtype=jnp.int32)
    path = at // (group // 2)
    outer = at // (group // 2 // ny) % ny
    inner = at // block % nx
    behind_y = jnp.where(path == 0, outer, inner)
    behind_x = jnp.where(path == 0, inner, outer)
    place = ((y - behind_y) % ny * nx + (x - behind_x) % nx) * 2 + path
    place = place * block + at % block
    order = (place[:, None] == jnp.arange(group, dtype=jnp.int32)[None, :]).astype(F32)

    def flipped(array):
        halves = array.reshape(-1, 2, block)
        return jnp.where(h == 0, halves, halves[:, ::-1]).reshape(array.shape)

    along_x = around(hidden, "x")
    both = jnp.concatenate([hidden, cotangent])
    near = swap(both, "h")
    far = [swap(both, "za"), lax.ppermute(both, ("za", "h"), [(0, 3), (3, 0), (1, 2), (2, 1)])]
    along_y = jnp.concatenate(around(near[:block], "y"))
    far = [after(blocks_of, along_y) for blocks_of in far]
    sends = [far[0][:block], far[1][:block], far[0][block:], far[1][block:], cotangent, near[block:]]
    ids = flipped(jnp.stack([input_ids, target_ids]))
    local_target = jnp.dot(order, ids[1].astype(F32), precision=EXACT).astype(jnp.int32)
    sends, along_x, along_y, order, local_target = lax.optimization_barrier(
        (jnp.concatenate(sends), jnp.concatenate(along_x), along_y, order, local_target)
    )
    more = lax.all_gather(sends, ("y", "x"), axis=0, tiled=True)

    rows = jnp.concatenate(around(along_x, "y") + around(along_y, "x"))

    logits = lax.dot_general(rows, table, (((1,), (1,)), ((), ())), preferred_element_type=F32)
    columns = offset + jnp.arange(shard_rows, dtype=jnp.int32)
    hit = local_target[:, None] == columns[None, :]
    local_pick = jnp.sum(jnp.where(hit, logits, F32(0.0)), axis=1)
    local_max = jnp.max(logits, axis=1)
    local_total = jnp.sum(jnp.exp(logits - local_max[:, None]), axis=1)
    mine = jnp.dot(jnp.stack([local_max, local_total, local_pick]), order, precision=EXACT)
    mine_all = jnp.broadcast_to(flipped(mine), (lax.axis_size(VOCAB), *mine.shape))
    everyone = lax.all_to_all(mine_all, VOCAB, 0, 0, tiled=True)

    ids = after(ids, mine_all)
    own_in, own_target = ids
    other_in, other_target = swap(ids, "za")

    weights = jnp.exp(logits - after(local_max, mine_all)[:, None]).astype(BF16)
    weights = jnp.dot(order.T.astype(BF16), weights, preferred_element_type=F32).astype(BF16)
    chips, quarter = ny * nx, half_rows // 4
    blocks = jnp.stack([2 * zb + c, 2 - 2 * zb + c, 2 * zb + 1 - c, 3 - 2 * zb - c])
    within = jnp.arange(half_rows, dtype=jnp.int32)
    wanted = blocks[within // quarter] * quarter + within % quarter
    choose = lambda side: (
        jnp.arange(shard_rows, dtype=jnp.int32)[:, None] == side * half_rows + wanted[None, :]
    ).astype(BF16)
    pick_columns = lambda array, side: jnp.dot(array, side, preferred_element_type=F32).astype(BF16)
    own_side, other_side = lax.optimization_barrier((choose(za), choose(1 - za)))
    for_other = pick_columns(weights, other_side)
    other_weights = swap(for_other, "za")
    weights, own_side = lax.optimization_barrier((weights, own_side, for_other))[:2]
    summed, target_rows = hidden_product(
        weights, (own_target[:, None] == columns[None, :]).astype(BF16), table
    )
    half_columns = offset + half + wanted
    picks = [(ids[:, None] == half_columns[None, :]).astype(BF16) for ids in (other_in, own_in)]
    picks = jnp.concatenate([part.reshape(chips, 2 * block, half_rows) for part in picks], axis=1)
    picks = picks.reshape(-1, half_rows)

    top = jnp.max(everyone[:, 0], axis=0)
    total = jnp.sum(everyone[:, 1] * jnp.exp(everyone[:, 0] - top), axis=0)
    lse = top + jnp.log(total)
    token_loss = lse - jnp.sum(everyone[:, 2], axis=0)
    lse = flipped(lse)
    scale = jnp.exp(mine[0] - lse)
    lse_local = jnp.dot(order, lse, precision=EXACT)

    partial = (summed * scale[:, None] - target_rows.astype(F32)).astype(BF16)
    other_scale = swap(after(scale, partial), "za")
    lse_local = after(lse_local, partial)
    partial = lax.all_to_all(partial, ("y", "x"), 0, 0, tiled=True)

    dlogits = (jnp.exp(logits - lse_local[:, None]) - hit.astype(F32)).astype(BF16)
    own_dlogits = pick_columns(dlogits, own_side)
    other_hit = (other_target[:, None] == half_columns[None, :]).astype(F32)
    other_dlogits = (other_weights.astype(F32) * other_scale[:, None] - other_hit).astype(BF16)
    pieces = []
    for at_column in range(0, width, width // CHUNKS):
        keep, send = table_product(
            own_dlogits, other_dlogits, picks, rows, more, at_column, width // CHUNKS
        )
        own_dlogits = after(own_dlogits, send)
        got = swap(send, "c")
        mine, theirs = (k + g.astype(F32) for k, g in zip(cut(keep, 2), cut(got, 2)))
        pieces.append((mine, theirs.astype(BF16)))

    partial = after(partial, pieces[-1][1])
    parts = jnp.sum(partial.reshape(chips, 2, block, width).astype(F32), axis=0)
    last = [swap(theirs, "zb") for _, theirs in pieces]
    near_part = swap(after(parts[1], *(theirs for _, theirs in pieces)), "h")
    near_part, *last = lax.optimization_barrier((near_part, *last))
    hidden_grad = (parts[0] + near_part).astype(BF16)
    table_grad = jnp.concatenate(
        [mine + got.astype(F32) for (mine, _), got in zip(pieces, last)], axis=1
    )
    return (table_grad, hidden_grad, token_loss)


def solution(mesh):
    finer = Mesh(mesh.devices.reshape(2, 2, 2, 4, 4, 2), DP + VOCAB)
    in_specs = (P(VOCAB, None), P(DP + VOCAB, None), P(DP + VOCAB, None), P(DP), P(DP))
    out_specs = (P(VOCAB + DP, None), P(DP + VOCAB, None), P(DP))
    return jax.shard_map(
        shards, mesh=finer, in_specs=in_specs, out_specs=out_specs, check_vma=False
    )
```

```python
import functools

import jax
import jax.numpy as jnp
from jax import lax
from jax.experimental import pallas as pl
from jax.experimental.pallas import tpu as pltpu
from jax.sharding import Mesh
from jax.sharding import PartitionSpec as P

VOCAB = ("y", "x", "h")
DP = ("za", "zb", "c")
F32 = jnp.float32
BF16 = jnp.bfloat16
CHUNKS = 2
EXACT = lax.Precision.HIGHEST


def after(value, *others):
    return lax.optimization_barrier((value, *others))[0]


def shift(array, axis, by):
    n = lax.axis_size(axis)
    return lax.ppermute(array, axis, [(i, (i + by) % n) for i in range(n)])


def swap(array, axis):
    n = lax.axis_size(axis)
    return lax.ppermute(array, axis, [(i, n - 1 - i) for i in range(n)])


def hidden_product_kernel(weights_ref, hit_ref, table_ref, sum_ref, target_ref):
    left = jnp.concatenate([weights_ref[...], hit_ref[...]])
    both = jnp.dot(left, table_ref[...], preferred_element_type=F32)
    tokens = sum_ref.shape[0]
    sum_ref[...] = both[:tokens]
    target_ref[...] = both[tokens:].astype(BF16)


def hidden_product(weights, hit, table):
    tokens, depth = weights.shape
    columns = table.shape[1]
    tile = min(512, columns)
    still = pl.BlockSpec((tokens, depth), lambda i: (0, 0))
    out = pl.BlockSpec((tokens, tile), lambda i: (0, i))
    return pl.pallas_call(
        hidden_product_kernel,
        grid=(columns // tile,),
        in_specs=[still, still, pl.BlockSpec((depth, tile), lambda i: (0, i))],
        out_specs=[out, out],
        out_shape=[jax.ShapeDtypeStruct((tokens, columns), kind) for kind in (F32, BF16)],
        compiler_params=pltpu.CompilerParams(vmem_limit_bytes=56 << 20),
        cost_estimate=pl.CostEstimate(
            flops=4 * tokens * depth * columns,
            bytes_accessed=2 * depth * (2 * tokens + columns) + 6 * tokens * columns,
            transcendentals=0,
        ),
    )(weights, hit, table)


def table_product_kernel(chips, own_ref, other_ref, picks_ref, rows_ref, more_ref, keep_ref, send_ref):
    contract = (((0,), (0,)), ((), ()))
    tile = more_ref.shape[1]
    more = more_ref[...].reshape(chips, -1, tile)
    split = other_ref.shape[0] // chips
    total = lax.dot_general(own_ref[...], rows_ref[...], contract, preferred_element_type=F32)
    for left, right in ((other_ref, more[:, :split]), (picks_ref, more[:, split:])):
        right = right.reshape(-1, tile)
        total += lax.dot_general(left[...], right, contract, preferred_element_type=F32)
    half = total.shape[0] // 2
    keep_ref[...] = total[:half]
    send_ref[...] = total[half:].astype(BF16)


def table_product(own, other, picks, rows, more, at_column, columns):
    tokens, out_rows = own.shape
    depth = more.shape[0]
    chips = lax.axis_size(("y", "x"))
    tile = min(512, columns)
    begin = at_column // tile
    still = lambda i: (0, 0)
    moving = lambda i: (0, begin + i)
    return pl.pallas_call(
        functools.partial(table_product_kernel, chips),
        grid=(columns // tile,),
        in_specs=[
            pl.BlockSpec((tokens, out_rows), still),
            pl.BlockSpec((tokens, out_rows), still),
            pl.BlockSpec((depth - tokens, out_rows), still),
            pl.BlockSpec((tokens, tile), moving),
            pl.BlockSpec((depth, tile), moving),
        ],
        out_specs=[pl.BlockSpec((out_rows // 2, tile), lambda i: (0, i))] * 2,
        out_shape=[
            jax.ShapeDtypeStruct((out_rows // 2, columns), F32),
            jax.ShapeDtypeStruct((out_rows // 2, columns), BF16),
        ],
        compiler_params=pltpu.CompilerParams(vmem_limit_bytes=56 << 20),
        cost_estimate=pl.CostEstimate(
            flops=2 * (tokens + depth) * out_rows * columns,
            bytes_accessed=2 * (tokens + depth) * (out_rows + columns) + 3 * out_rows * columns,
            transcendentals=0,
        ),
    )(own, other, picks, rows, more)


def around(array, axis):
    return [array] + [shift(array, axis, k) for k in range(1, lax.axis_size(axis))]


def cut(array, count):
    size = array.shape[0] // count
    return [array[k * size : (k + 1) * size] for k in range(count)]


def shards(table, hidden, cotangent, input_ids, target_ids):
    shard_rows, width = table.shape
    block = hidden.shape[0]
    group = input_ids.shape[0]
    half_rows = shard_rows // 2
    y, x, h = (lax.axis_index(name) for name in VOCAB)
    za, zb, c = (lax.axis_index(name) for name in DP)
    ny, nx = lax.axis_size("y"), lax.axis_size("x")
    offset = lax.axis_index(VOCAB) * shard_rows
    half = za * half_rows

    at = jnp.arange(group, dtype=jnp.int32)
    path = at // (group // 2)
    outer = at // (group // 2 // ny) % ny
    inner = at // block % nx
    behind_y = jnp.where(path == 0, outer, inner)
    behind_x = jnp.where(path == 0, inner, outer)
    place = ((y - behind_y) % ny * nx + (x - behind_x) % nx) * 2 + path
    place = place * block + at % block
    order = (place[:, None] == jnp.arange(group, dtype=jnp.int32)[None, :]).astype(F32)

    def flipped(array):
        halves = array.reshape(-1, 2, block)
        return jnp.where(h == 0, halves, halves[:, ::-1]).reshape(array.shape)

    along_x = around(hidden, "x")
    both = jnp.concatenate([hidden, cotangent])
    near = swap(both, "h")
    far = [swap(both, "za"), lax.ppermute(both, ("za", "h"), [(0, 3), (3, 0), (1, 2), (2, 1)])]
    along_y = jnp.concatenate(around(near[:block], "y"))
    far = [after(blocks_of, along_y) for blocks_of in far]
    sends = [far[0][:block], far[1][:block], far[0][block:], far[1][block:], cotangent, near[block:]]
    ids = flipped(jnp.stack([input_ids, target_ids]))
    local_target = jnp.dot(order, ids[1].astype(F32), precision=EXACT).astype(jnp.int32)
    sends, along_x, along_y, order, local_target = lax.optimization_barrier(
        (jnp.concatenate(sends), jnp.concatenate(along_x), along_y, order, local_target)
    )
    more = lax.all_gather(sends, ("y", "x"), axis=0, tiled=True)

    rows = jnp.concatenate(around(along_x, "y") + around(along_y, "x"))

    logits = lax.dot_general(rows, table, (((1,), (1,)), ((), ())), preferred_element_type=F32)
    columns = offset + jnp.arange(shard_rows, dtype=jnp.int32)
    hit = local_target[:, None] == columns[None, :]
    local_pick = jnp.sum(jnp.where(hit, logits, F32(0.0)), axis=1)
    local_max = jnp.max(logits, axis=1)
    local_total = jnp.sum(jnp.exp(logits - local_max[:, None]), axis=1)
    mine = jnp.dot(jnp.stack([local_max, local_total, local_pick]), order, precision=EXACT)
    mine_all = jnp.broadcast_to(flipped(mine), (lax.axis_size(VOCAB), *mine.shape))
    everyone = lax.all_to_all(mine_all, VOCAB, 0, 0, tiled=True)

    ids = after(ids, mine_all)
    own_in, own_target = ids
    other_in, other_target = swap(ids, "za")

    weights = jnp.exp(logits - after(local_max, mine_all)[:, None]).astype(BF16)
    weights = jnp.dot(order.T.astype(BF16), weights, preferred_element_type=F32).astype(BF16)
    chips, quarter = ny * nx, half_rows // 4
    blocks = jnp.stack([2 * zb + c, 2 - 2 * zb + c, 2 * zb + 1 - c, 3 - 2 * zb - c])
    within = jnp.arange(half_rows, dtype=jnp.int32)
    wanted = blocks[within // quarter] * quarter + within % quarter
    choose = lambda side: (
        jnp.arange(shard_rows, dtype=jnp.int32)[:, None] == side * half_rows + wanted[None, :]
    ).astype(BF16)
    pick_columns = lambda array, side: jnp.dot(array, side, preferred_element_type=F32).astype(BF16)
    own_side, other_side = lax.optimization_barrier((choose(za), choose(1 - za)))
    for_other = pick_columns(weights, other_side)
    other_weights = swap(for_other, "za")
    weights, own_side = lax.optimization_barrier((weights, own_side, for_other))[:2]
    summed, target_rows = hidden_product(
        weights, (own_target[:, None] == columns[None, :]).astype(BF16), table
    )
    half_columns = offset + half + wanted
    picks = [(ids[:, None] == half_columns[None, :]).astype(BF16) for ids in (other_in, own_in)]
    picks = jnp.concatenate([part.reshape(chips, 2 * block, half_rows) for part in picks], axis=1)
    picks = picks.reshape(-1, half_rows)

    top = jnp.max(everyone[:, 0], axis=0)
    total = jnp.sum(everyone[:, 1] * jnp.exp(everyone[:, 0] - top), axis=0)
    lse = top + jnp.log(total)
    token_loss = lse - jnp.sum(everyone[:, 2], axis=0)
    lse = flipped(lse)
    scale = jnp.exp(mine[0] - lse)
    lse_local = jnp.dot(order, lse, precision=EXACT)

    partial = (summed * scale[:, None] - target_rows.astype(F32)).astype(BF16)
    other_scale = swap(after(scale, partial), "za")
    lse_local = after(lse_local, partial)
    partial = lax.all_to_all(partial, ("y", "x"), 0, 0, tiled=True)

    dlogits = (jnp.exp(logits - lse_local[:, None]) - hit.astype(F32)).astype(BF16)
    own_dlogits = pick_columns(dlogits, own_side)
    other_hit = (other_target[:, None] == half_columns[None, :]).astype(F32)
    other_dlogits = (other_weights.astype(F32) * other_scale[:, None] - other_hit).astype(BF16)
    pieces = []
    for at_column in range(0, width, width // CHUNKS):
        keep, send = table_product(
            own_dlogits, other_dlogits, picks, rows, more, at_column, width // CHUNKS
        )
        own_dlogits = after(own_dlogits, send)
        got = swap(send, "c")
        mine, theirs = (k + g.astype(F32) for k, g in zip(cut(keep, 2), cut(got, 2)))
        theirs = theirs.astype(BF16)
        pieces.append((mine, swap(theirs, "zb")))
    table_grad = jnp.concatenate([mine + last.astype(F32) for mine, last in pieces], axis=1)

    partial = after(partial, theirs)
    parts = jnp.sum(partial.reshape(chips, 2, block, width).astype(F32), axis=0)
    hidden_grad = (parts[0] + swap(parts[1], "h")).astype(BF16)
    return (table_grad, hidden_grad, token_loss)


def solution(mesh):
    finer = Mesh(mesh.devices.reshape(2, 2, 2, 4, 4, 2), DP + VOCAB)
    in_specs = (P(VOCAB, None), P(DP + VOCAB, None), P(DP + VOCAB, None), P(DP), P(DP))
    out_specs = (P(VOCAB + DP, None), P(DP + VOCAB, None), P(DP))
    return jax.shard_map(
        shards, mesh=finer, in_specs=in_specs, out_specs=out_specs, check_vma=False
    )
```

```python
import functools

import jax
import jax.numpy as jnp
from jax import lax
from jax.experimental import pallas as pl
from jax.experimental.pallas import tpu as pltpu
from jax.sharding import Mesh
from jax.sharding import PartitionSpec as P

VOCAB = ("y", "x", "h")
DP = ("za", "zb", "c")
F32 = jnp.float32
BF16 = jnp.bfloat16
CHUNKS = 2
EXACT = lax.Precision.HIGHEST


def after(value, *others):
    return lax.optimization_barrier((value, *others))[0]


def shift(array, axis, by):
    n = lax.axis_size(axis)
    return lax.ppermute(array, axis, [(i, (i + by) % n) for i in range(n)])


def swap(array, axis):
    n = lax.axis_size(axis)
    return lax.ppermute(array, axis, [(i, n - 1 - i) for i in range(n)])


def hidden_product_kernel(weights_ref, hit_ref, table_ref, sum_ref, target_ref):
    left = jnp.concatenate([weights_ref[...], hit_ref[...]])
    both = jnp.dot(left, table_ref[...], preferred_element_type=F32)
    tokens = sum_ref.shape[0]
    sum_ref[...] = both[:tokens]
    target_ref[...] = both[tokens:].astype(BF16)


def hidden_product(weights, hit, table):
    tokens, depth = weights.shape
    columns = table.shape[1]
    tile = min(1024, columns)
    still = pl.BlockSpec((tokens, depth), lambda i: (0, 0))
    out = pl.BlockSpec((tokens, tile), lambda i: (0, i))
    return pl.pallas_call(
        hidden_product_kernel,
        grid=(columns // tile,),
        in_specs=[still, still, pl.BlockSpec((depth, tile), lambda i: (0, i))],
        out_specs=[out, out],
        out_shape=[jax.ShapeDtypeStruct((tokens, columns), kind) for kind in (F32, BF16)],
        compiler_params=pltpu.CompilerParams(vmem_limit_bytes=56 << 20),
        cost_estimate=pl.CostEstimate(
            flops=4 * tokens * depth * columns,
            bytes_accessed=2 * depth * (2 * tokens + columns) + 6 * tokens * columns,
            transcendentals=0,
        ),
    )(weights, hit, table)


def table_product_kernel(chips, own_ref, other_ref, picks_ref, rows_ref, more_ref, keep_ref, send_ref):
    contract = (((0,), (0,)), ((), ()))
    tile = more_ref.shape[1]
    more = more_ref[...].reshape(chips, -1, tile)
    split = other_ref.shape[0] // chips
    total = lax.dot_general(own_ref[...], rows_ref[...], contract, preferred_element_type=F32)
    for left, right in ((other_ref, more[:, :split]), (picks_ref, more[:, split:])):
        right = right.reshape(-1, tile)
        total += lax.dot_general(left[...], right, contract, preferred_element_type=F32)
    half = total.shape[0] // 2
    keep_ref[...] = total[:half]
    send_ref[...] = total[half:].astype(BF16)


def table_product(own, other, picks, rows, more, at_column, columns):
    tokens, out_rows = own.shape
    depth = more.shape[0]
    chips = lax.axis_size(("y", "x"))
    tile = min(1024, columns)
    begin = at_column // tile
    still = lambda i: (0, 0)
    moving = lambda i: (0, begin + i)
    return pl.pallas_call(
        functools.partial(table_product_kernel, chips),
        grid=(columns // tile,),
        in_specs=[
            pl.BlockSpec((tokens, out_rows), still),
            pl.BlockSpec((tokens, out_rows), still),
            pl.BlockSpec((depth - tokens, out_rows), still),
            pl.BlockSpec((tokens, tile), moving),
            pl.BlockSpec((depth, tile), moving),
        ],
        out_specs=[pl.BlockSpec((out_rows // 2, tile), lambda i: (0, i))] * 2,
        out_shape=[
            jax.ShapeDtypeStruct((out_rows // 2, columns), F32),
            jax.ShapeDtypeStruct((out_rows // 2, columns), BF16),
        ],
        compiler_params=pltpu.CompilerParams(vmem_limit_bytes=56 << 20),
        cost_estimate=pl.CostEstimate(
            flops=2 * (tokens + depth) * out_rows * columns,
            bytes_accessed=2 * (tokens + depth) * (out_rows + columns) + 3 * out_rows * columns,
            transcendentals=0,
        ),
    )(own, other, picks, rows, more)


def around(array, axis):
    return [array] + [shift(array, axis, k) for k in range(1, lax.axis_size(axis))]


def cut(array, count):
    size = array.shape[0] // count
    return [array[k * size : (k + 1) * size] for k in range(count)]


def shards(table, hidden, cotangent, input_ids, target_ids):
    shard_rows, width = table.shape
    block = hidden.shape[0]
    group = input_ids.shape[0]
    half_rows = shard_rows // 2
    y, x, h = (lax.axis_index(name) for name in VOCAB)
    za, zb, c = (lax.axis_index(name) for name in DP)
    ny, nx = lax.axis_size("y"), lax.axis_size("x")
    offset = lax.axis_index(VOCAB) * shard_rows
    half = za * half_rows

    at = jnp.arange(group, dtype=jnp.int32)
    path = at // (group // 2)
    outer = at // (group // 2 // ny) % ny
    inner = at // block % nx
    behind_y = jnp.where(path == 0, outer, inner)
    behind_x = jnp.where(path == 0, inner, outer)
    place = ((y - behind_y) % ny * nx + (x - behind_x) % nx) * 2 + path
    place = place * block + at % block
    order = (place[:, None] == jnp.arange(group, dtype=jnp.int32)[None, :]).astype(F32)

    def flipped(array):
        halves = array.reshape(-1, 2, block)
        return jnp.where(h == 0, halves, halves[:, ::-1]).reshape(array.shape)

    along_x = around(hidden, "x")
    both = jnp.concatenate([hidden, cotangent])
    near = swap(both, "h")
    far = [swap(both, "za"), lax.ppermute(both, ("za", "h"), [(0, 3), (3, 0), (1, 2), (2, 1)])]
    along_y = jnp.concatenate(around(near[:block], "y"))
    far = [after(blocks_of, along_y) for blocks_of in far]
    sends = [far[0][:block], far[1][:block], far[0][block:], far[1][block:], cotangent, near[block:]]
    ids = flipped(jnp.stack([input_ids, target_ids]))
    local_target = jnp.dot(order, ids[1].astype(F32), precision=EXACT).astype(jnp.int32)
    sends, along_x, along_y, order, local_target = lax.optimization_barrier(
        (jnp.concatenate(sends), jnp.concatenate(along_x), along_y, order, local_target)
    )
    more = lax.all_gather(sends, ("y", "x"), axis=0, tiled=True)

    rows = jnp.concatenate(around(along_x, "y") + around(along_y, "x"))

    logits = lax.dot_general(rows, table, (((1,), (1,)), ((), ())), preferred_element_type=F32)
    columns = offset + jnp.arange(shard_rows, dtype=jnp.int32)
    hit = local_target[:, None] == columns[None, :]
    local_pick = jnp.sum(jnp.where(hit, logits, F32(0.0)), axis=1)
    local_max = jnp.max(logits, axis=1)
    local_total = jnp.sum(jnp.exp(logits - local_max[:, None]), axis=1)
    mine = jnp.dot(jnp.stack([local_max, local_total, local_pick]), order, precision=EXACT)
    mine_all = jnp.broadcast_to(flipped(mine), (lax.axis_size(VOCAB), *mine.shape))
    everyone = lax.all_to_all(mine_all, VOCAB, 0, 0, tiled=True)

    ids = after(ids, mine_all)
    own_in, own_target = ids
    other_in, other_target = swap(ids, "za")

    weights = jnp.exp(logits - after(local_max, mine_all)[:, None]).astype(BF16)
    weights = jnp.dot(order.T.astype(BF16), weights, preferred_element_type=F32).astype(BF16)
    chips, quarter = ny * nx, half_rows // 4
    blocks = jnp.stack([2 * zb + c, 2 - 2 * zb + c, 2 * zb + 1 - c, 3 - 2 * zb - c])
    within = jnp.arange(half_rows, dtype=jnp.int32)
    wanted = blocks[within // quarter] * quarter + within % quarter
    choose = lambda side: (
        jnp.arange(shard_rows, dtype=jnp.int32)[:, None] == side * half_rows + wanted[None, :]
    ).astype(BF16)
    pick_columns = lambda array, side: jnp.dot(array, side, preferred_element_type=F32).astype(BF16)
    own_side, other_side = lax.optimization_barrier((choose(za), choose(1 - za)))
    for_other = pick_columns(weights, other_side)
    other_weights = swap(for_other, "za")
    weights, own_side = lax.optimization_barrier((weights, own_side, for_other))[:2]
    summed, target_rows = hidden_product(
        weights, (own_target[:, None] == columns[None, :]).astype(BF16), table
    )
    half_columns = offset + half + wanted
    picks = [(ids[:, None] == half_columns[None, :]).astype(BF16) for ids in (other_in, own_in)]
    picks = jnp.concatenate([part.reshape(chips, 2 * block, half_rows) for part in picks], axis=1)
    picks = picks.reshape(-1, half_rows)

    top = jnp.max(everyone[:, 0], axis=0)
    total = jnp.sum(everyone[:, 1] * jnp.exp(everyone[:, 0] - top), axis=0)
    lse = top + jnp.log(total)
    token_loss = lse - jnp.sum(everyone[:, 2], axis=0)
    lse = flipped(lse)
    scale = jnp.exp(mine[0] - lse)
    lse_local = jnp.dot(order, lse, precision=EXACT)

    partial = (summed * scale[:, None] - target_rows.astype(F32)).astype(BF16)
    other_scale = swap(after(scale, partial), "za")
    lse_local = after(lse_local, partial)
    partial = lax.all_to_all(partial, ("y", "x"), 0, 0, tiled=True)

    dlogits = (jnp.exp(logits - lse_local[:, None]) - hit.astype(F32)).astype(BF16)
    own_dlogits = pick_columns(dlogits, own_side)
    other_hit = (other_target[:, None] == half_columns[None, :]).astype(F32)
    other_dlogits = (other_weights.astype(F32) * other_scale[:, None] - other_hit).astype(BF16)
    pieces = []
    for at_column in range(0, width, width // CHUNKS):
        keep, send = table_product(
            own_dlogits, other_dlogits, picks, rows, more, at_column, width // CHUNKS
        )
        own_dlogits = after(own_dlogits, send)
        got = swap(send, "c")
        mine, theirs = (k + g.astype(F32) for k, g in zip(cut(keep, 2), cut(got, 2)))
        theirs = theirs.astype(BF16)
        pieces.append((mine, swap(theirs, "zb")))
    table_grad = jnp.concatenate([mine + last.astype(F32) for mine, last in pieces], axis=1)

    partial = after(partial, theirs)
    parts = jnp.sum(partial.reshape(chips, 2, block, width).astype(F32), axis=0)
    hidden_grad = (parts[0] + swap(parts[1], "h")).astype(BF16)
    return (table_grad, hidden_grad, token_loss)


def solution(mesh):
    finer = Mesh(mesh.devices.reshape(2, 2, 2, 4, 4, 2), DP + VOCAB)
    in_specs = (P(VOCAB, None), P(DP + VOCAB, None), P(DP + VOCAB, None), P(DP), P(DP))
    out_specs = (P(VOCAB + DP, None), P(DP + VOCAB, None), P(DP))
    return jax.shard_map(
        shards, mesh=finer, in_specs=in_specs, out_specs=out_specs, check_vma=False
    )
```
